1024 devices in a mesh: ctx: 256 (over z_hi, x, y, core), head: 4 (over z_lo).
Axes of the slice: x: 8, y: 8, z: 8 (z_hi: 2, z_lo: 4; z = z_hi * 4 + z_lo), core: 2. Of those that a mesh axis runs over, the one named last changes fastest.
Arguments:
- queries: bfloat16 [256, 256, 32, 128], P('ctx', 'head'), may hold values from -6 to 6
- keys: bfloat16 [256, 256, 4, 128], P('ctx', 'head'), may hold values from -6 to 6
- values: bfloat16 [256, 256, 4, 128], P('ctx', 'head'), may hold values from -6 to 6
Outputs:
- weighted: float32 [256, 256, 32, 128], P('ctx', None, 'head')
- row_max: float32 [32, 256, 256], P('head', 'ctx')
- row_sum: float32 [32, 256, 256], P('head', 'ctx')
The draws below stay inside these ranges and needn't reach their ends.
All inputs are finite; a program needn't handle non-finite values.
Results may differ from the reference program's by a relative error of at most 0.0027.
Values may be sent and summed in bfloat16 or wider, within the bound.
A program may use at most 32 MiB of HBM per device.

```python
import math
import jax
import jax.numpy as jnp
from jax import lax

HEAD_WIDTH = 128
QUERY_HEADS = 32
KEY_VALUE_HEADS = 4
WIN = 8
SUBBLOCK_TOKENS = 128
PAIRS = 256
SEQUENCE_TOKENS = 65536


def paired_draw(key):
    key_query = jax.random.fold_in(key, 11)
    key_random_seed = jax.random.fold_in(key, 12)
    query_entries = jax.random.truncated_normal(key_query, -6.0, 6.0, (SEQUENCE_TOKENS, QUERY_HEADS, HEAD_WIDTH), jnp.float32)
    key_entries = jax.random.truncated_normal(key_random_seed, -6.0, 6.0, (SEQUENCE_TOKENS, KEY_VALUE_HEADS, HEAD_WIDTH), jnp.float32)
    query_entries = query_entries.reshape(PAIRS, 2 * SUBBLOCK_TOKENS, QUERY_HEADS, HEAD_WIDTH)
    key_entries = key_entries.reshape(PAIRS, 2 * SUBBLOCK_TOKENS, KEY_VALUE_HEADS, HEAD_WIDTH)
    return (query_entries, key_entries)


def draw_queries(key, part):
    return paired_draw(key)[0].astype(jnp.bfloat16)


def draw_keys(key, part):
    return paired_draw(key)[1].astype(jnp.bfloat16)


def level_of(stream_key, dims, cuts, least, largest):
    def one(axis_at, blocks):
        heights = jax.random.uniform(jax.random.fold_in(jax.random.fold_in(stream_key, 6), axis_at), (blocks,), jnp.float32, least / len(cuts), largest / len(cuts))
        return jnp.repeat(jnp.exp(heights), dims[axis_at] // blocks).reshape((-1,) + (1,) * (len(dims) - axis_at - 1))

    level = one(*cuts[0])
    for cut in cuts[1:]:
        level = level * one(*cut)
    return level


def gaussian(stream_key, shape, scale, most, shards=(), kind=jnp.bfloat16):
    level = level_of(stream_key, shape, shards, -0.22, 0.18) if shards else 1.0
    array = jax.random.normal(stream_key, shape, jnp.float32) * scale * level
    return jnp.minimum(jnp.maximum(array, -most), most).astype(kind)


def setup_inputs(seed: int = 0) -> dict:
    seeds = jax.random.split(jax.random.key(seed), 4)
    queries = draw_queries(jax.random.fold_in(seeds[3], 71), 0)
    keys = draw_keys(jax.random.fold_in(seeds[3], 71), 0)
    values = gaussian(seeds[2], (PAIRS, 2 * SUBBLOCK_TOKENS, KEY_VALUE_HEADS, HEAD_WIDTH), 1.0, 6.0, ((0, 256), (1, 4)))
    return {"queries": queries, "keys": keys, "values": values}


def reference(queries, keys, values):
    period_length = PAIRS
    row_halves = SUBBLOCK_TOKENS
    query_group_count = QUERY_HEADS // KEY_VALUE_HEADS
    score_scale = 1.0 / math.sqrt(HEAD_WIDTH)
    row_ids = jnp.arange(row_halves, dtype=jnp.int32)

    def positions(pair_id):
        subs = jnp.stack([2 * pair_id, 2 * period_length - 1 - 2 * pair_id]).astype(jnp.int32)
        return (subs[:, None] * row_halves + row_ids[None, :]).reshape(-1)

    def one_pair(pair_id):
        query_rows = lax.dynamic_index_in_dim(queries, pair_id, 0, keepdims=False).astype(jnp.float32)
        pos_q = positions(pair_id)
        sources = ((pair_id - jnp.arange(WIN, dtype=jnp.int32)) % period_length).astype(jnp.int32)
        pos_k = jax.vmap(positions)(sources).reshape(-1)
        key_row_block = jnp.take(keys, sources, axis=0).reshape(-1, KEY_VALUE_HEADS, HEAD_WIDTH).astype(jnp.float32)
        value_row_block = jnp.take(values, sources, axis=0).reshape(-1, KEY_VALUE_HEADS, HEAD_WIDTH).astype(jnp.float32)
        key_row_block = jnp.repeat(key_row_block, query_group_count, axis=1)
        value_row_block = jnp.repeat(value_row_block, query_group_count, axis=1)
        scores = jnp.einsum('qhd,khd->hqk', query_rows, key_row_block) * score_scale
        visible = pos_k[None, None, :] <= pos_q[None, :, None]
        scores = jnp.where(visible, scores, jnp.float32(-1e+30))
        top_score = lax.optimization_barrier(jnp.max(scores, axis=2))
        weights = jnp.where(visible, jnp.exp(scores - top_score[:, :, None]), jnp.float32(0.0))
        total_weight = lax.optimization_barrier(jnp.sum(weights, axis=2))
        low_weights = weights.astype(jnp.bfloat16).astype(jnp.float32)
        combined = jnp.einsum('hqk,khd->qhd', low_weights, value_row_block)
        return (combined, top_score, total_weight)
    combined, top_score, total_weight = lax.map(one_pair, jnp.arange(period_length, dtype=jnp.int32))
    return (combined, jnp.transpose(top_score, (1, 0, 2)), jnp.transpose(total_weight, (1, 0, 2)))
```

```python
import functools
import math

import jax
import jax.numpy as jnp
from jax import lax
from jax.experimental import pallas as pl
from jax.experimental.pallas import tpu as pltpu
from jax.sharding import PartitionSpec as P

MESH = pl.DeviceIdType.MESH
HALF = 128
ROWS = 64
HEADS = 4
GROUP = 8
WIDTH = 128
BLOCK = 128
PAIRS = 256
WIN = 8


def gather_kernel(q_ref, k_ref, v_ref, q_out, x_out, wide, stage,
                  q_send, q_recv, q_own, s_send, s_recv, s_own, e_send, c_send, b_send, d_send, x_recv, w_send):
    c = lax.axis_index("ctx")
    h = lax.axis_index("head")
    core = lax.rem(c, 2)
    place = lax.rem(c, BLOCK)
    back = BLOCK - place
    crosser = back <= 7
    over = c >= BLOCK
    base = lax.select(over, 0, BLOCK)
    x_core = lax.select(back == 7, 0, lax.rem(back, 2))
    x_j = lax.select(back == 7, 7, back + lax.rem(back, 2))
    near = place < 2
    last = place >= BLOCK - 2
    sibling = c + 1 - 2 * core

    def wrapped(pair):
        return lax.rem(pair + PAIRS, PAIRS)

    bar = pltpu.get_barrier_semaphore()

    def greet(pair, head):
        pl.semaphore_signal(bar, inc=1, device_id=(pair, head), device_id_type=MESH)

    for s in range(1, HEADS):
        greet(c, lax.rem(h + s, HEADS))
    greet(sibling, h)

    @pl.when(jnp.logical_not(near))
    def _():
        greet(c - 2, h)

        @pl.when(core == 0)
        def _():
            greet(c - 1, h)

    @pl.when(near)
    def _():
        for j in (2, 4, 6, 7):
            @pl.when((j != 7) | (core == 0))
            def _():
                for r in range(HEADS):
                    greet(wrapped(c - j), r)

    for n, ref in enumerate((k_ref, v_ref)):
        wide[n] = ref[...].astype(jnp.float32)
    for n in range(2):
        for head in range(HEADS):
            stage[n, head] = wide[n, pl.ds(head, ROWS, stride=HEADS), :].astype(jnp.bfloat16)

    one, none = jnp.int32(1), jnp.int32(0)
    targets = (4 + lax.select(last, none, one) + lax.select(last | (core == 0), none, one)
               + lax.select(crosser, one, none) * 4)
    pl.semaphore_wait(bar, targets)

    def remote(src, dst, send, recv, pair, head):
        return pltpu.make_async_remote_copy(src_ref=src, dst_ref=dst, send_sem=send, recv_sem=recv,
                                            device_id=(pair, head), device_id_type=MESH)

    def own_rows(head):
        return x_out.at[:, head // 2, 0, pl.ds(lax.rem(head, 2) * ROWS, ROWS), :]

    kv_copies = []
    for s in (3, 2, 1):
        to = lax.rem(h + s, HEADS)
        copy = remote(stage.at[:, to], own_rows(h), s_send.at[s], s_recv.at[h], c, to)
        copy.start()
        kv_copies.append(copy)
    kv_own = pltpu.make_async_copy(stage.at[:, h], own_rows(h), s_own)
    kv_own.start()

    half_to = lax.select(over, 1 - h // 2, h // 2)

    def cross_copy(to):
        return remote(stage.at[:, to], x_out.at[:, half_to, x_j, pl.ds(lax.rem(h, 2) * ROWS, ROWS), :],
                      w_send.at[to], x_recv.at[x_j, half_to], base + x_core, to)

    @pl.when(crosser)
    def _():
        for to in range(HEADS):
            cross_copy(to).start()

    q_copies = []
    for s in (3, 2, 1):
        to = lax.rem(h + s, HEADS)
        copy = remote(q_ref.at[:, to], q_out.at[h], q_send.at[s], q_recv.at[h], c, to)
        copy.start()
        q_copies.append(copy)
    q_mine = pltpu.make_async_copy(q_ref.at[:, h], q_out.at[h], q_own)
    q_mine.start()

    kv_own.wait()

    def arrive(head):
        @pl.when(h != head)
        def _():
            remote(stage.at[:, head], own_rows(head), e_send, s_recv.at[head], c, h).wait_recv()

    def block(half, j):
        return x_out.at[:, half, j]

    def along(j, half):
        return remote(block(half, j), block(half, j + 2), c_send.at[j // 2, half], x_recv.at[j + 2, half],
                      wrapped(c + 2), h)

    def beside(j, half):
        j_to = j + 1 - 2 * core
        return remote(block(half, j), block(half, j_to), b_send.at[j // 2, half], x_recv.at[j_to, half], sibling, h)

    def ahead(half):
        return remote(block(half, 6), block(half, 7), d_send.at[half], x_recv.at[7, half], wrapped(c + 1), h)

    def landed(j, half):
        remote(block(half, j), block(half, j), e_send, x_recv.at[j, half], c, h).wait_recv()

    for j in (0, 2, 4, 6):
        for half in range(2):
            if j:
                landed(j, half)
            else:
                arrive(2 * half)
                arrive(2 * half + 1)
            if j < 6:
                @pl.when(jnp.logical_not(last))
                def _():
                    along(j, half).start()
            else:
                @pl.when(jnp.logical_not(last) & (core == 1))
                def _():
                    ahead(half).start()
            if j:
                beside(j, half).start()
            else:
                @pl.when(core == 0)
                def _():
                    beside(0, half).start()
    for j in (1, 3, 5, 7):
        for half in range(2):
            landed(j, half)
    for s in (1, 2, 3):
        head = lax.rem(h + s, HEADS)
        remote(q_ref.at[:, head], q_out.at[head], e_send, q_recv.at[head], c, h).wait_recv()
    q_mine.wait()
    for copy in kv_copies + q_copies:
        copy.wait_send()

    @pl.when(crosser)
    def _():
        for to in range(HEADS):
            cross_copy(to).wait_send()

    for half in range(2):
        @pl.when(jnp.logical_not(last))
        def _():
            for j in (0, 2, 4):
                along(j, half).wait_send()

        @pl.when(jnp.logical_not(last) & (core == 1))
        def _():
            ahead(half).wait_send()

        @pl.when(core == 0)
        def _():
            beside(0, half).wait_send()
        for j in (2, 4, 6):
            beside(j, half).wait_send()


def gather(q, k, v):
    dma = pltpu.SemaphoreType.DMA
    any_space = pl.BlockSpec(memory_space=pl.ANY)
    vmem = pl.BlockSpec(memory_space=pltpu.VMEM)
    return pl.pallas_call(
        gather_kernel,
        out_shape=(
            jax.ShapeDtypeStruct((HEADS, ROWS, GROUP, WIDTH), jnp.bfloat16),
            jax.ShapeDtypeStruct((2, 2, WIN, HALF, WIDTH), jnp.bfloat16),
        ),
        in_specs=[any_space, vmem, vmem],
        out_specs=(any_space, any_space),
        scratch_shapes=[
            pltpu.VMEM((2, ROWS * HEADS, WIDTH), jnp.float32),
            pltpu.VMEM((2, HEADS, ROWS, WIDTH), jnp.bfloat16),
            dma((4,)), dma((4,)), dma(()), dma((4,)), dma((4,)), dma(()), dma(()), dma((3, 2)), dma((4, 2)), dma((2,)),
            dma((8, 2)), dma((4,)),
        ],
        compiler_params=pltpu.CompilerParams(collective_id=0, has_side_effects=True),
        name="gather",
    )(q, k, v)


CHUNK = 256
TOKENS = CHUNK // GROUP
SCALE = 1.0 / math.sqrt(WIDTH)
LOG2E = math.log2(math.e)
LOW = -1e30


def nt_dot(a, b):
    return lax.dot_general(a, b, (((1,), (1,)), ((), ())), preferred_element_type=jnp.float32)


def attend_kernel(q_ref, x_ref, o_ref, m_ref, l_ref, stats):
    step = pl.program_id(0)
    half_steps = HALF // TOKENS
    c = lax.axis_index("ctx")
    token0 = lax.rem(step, half_steps) * TOKENS
    half = step // half_steps
    upper = c >= BLOCK
    place = lax.rem(c, BLOCK)
    special = place < 4
    q = q_ref[...]

    @pl.when(step == 0)
    def _():
        stats[...] = jnp.zeros_like(stats)

    def causal():
        row = token0 + lax.broadcasted_iota(jnp.int32, (CHUNK, HALF), 0) // GROUP
        return lax.broadcasted_iota(jnp.int32, (CHUNK, HALF), 1) <= row

    def put_stats(peak, norm):
        lane = lax.broadcasted_iota(jnp.int32, (TOKENS, GROUP, HALF), 2)
        want = token0 + lax.broadcasted_iota(jnp.int32, (TOKENS, GROUP, HALF), 0)
        hit = lane == want
        for n, value in enumerate((peak, norm)):
            wide = jnp.broadcast_to(value, (CHUNK, HALF)).reshape(TOKENS, GROUP, HALF)
            stats[n, half] += jnp.sum(jnp.where(hit, wide, 0.0), axis=0)

    def whole(diagonal, *ranges):
        pieces = [(diagonal, diagonal + 1), *(r for r in ranges if r[1] > r[0])]
        s = []
        for n, (a, b) in enumerate(pieces):
            one = nt_dot(q, x_ref[0, a:b].reshape(-1, WIDTH))
            s.append(one if n else jnp.where(causal(), one, LOW))
        peak = functools.reduce(jnp.maximum, [jnp.max(one, axis=1, keepdims=True) for one in s])
        norm, out = 0.0, 0.0
        for one, (a, b) in zip(s, pieces):
            p = jnp.exp2((one - peak) * (SCALE * LOG2E))
            norm += jnp.sum(p, axis=1, keepdims=True)
            out += jnp.dot(p.astype(jnp.bfloat16), x_ref[1, a:b].reshape(-1, WIDTH),
                           preferred_element_type=jnp.float32)
        o_ref[...] = out
        put_stats(peak * SCALE, norm)

    cases = {(0, None): ([(1, WIN)], [(0, WIN)]), (1, None): ([(1, 2 * WIN)], [])}
    for two in range(0, WIN, 2):
        cases[0, two // 2] = ([(1, two + 1)], [(0, WIN), (WIN + two + 1, 2 * WIN)])
        cases[1, two // 2] = ([(1, WIN + two + 1)], [(two + 1, WIN)])
    for (side, at), by_half in cases.items():
        here = (upper == (side == 1)) & (jnp.logical_not(special) if at is None else place == at)
        for which, ranges in enumerate(by_half):
            @pl.when(here & (half == which))
            def _():
                whole(which * WIN, *ranges)

    @pl.when(step == 2 * half_steps - 1)
    def _():
        for n, ref in enumerate((m_ref, l_ref)):
            for side in range(2):
                for g in range(GROUP):
                    ref[g, :, pl.ds(side * HALF, HALF)] = stats[n, side, pl.ds(g, 1), :]


def attend(q, x):
    rows = q.shape[0]
    return pl.pallas_call(
        attend_kernel,
        grid=(rows // CHUNK,),
        out_shape=(
            jax.ShapeDtypeStruct((rows, WIDTH), jnp.float32),
            jax.ShapeDtypeStruct((GROUP, 1, 2 * HALF), jnp.float32),
            jax.ShapeDtypeStruct((GROUP, 1, 2 * HALF), jnp.float32),
        ),
        in_specs=[
            pl.BlockSpec((CHUNK, WIDTH), lambda i: (i, 0)),
            pl.BlockSpec((2, 2 * WIN, HALF, WIDTH), lambda i: (0, 0, 0, 0)),
        ],
        out_specs=(
            pl.BlockSpec((CHUNK, WIDTH), lambda i: (i, 0)),
            pl.BlockSpec((GROUP, 1, 2 * HALF), lambda i: (0, 0, 0)),
            pl.BlockSpec((GROUP, 1, 2 * HALF), lambda i: (0, 0, 0)),
        ),
        scratch_shapes=[
            pltpu.VMEM((2, 2, GROUP, HALF), jnp.float32),
        ],
        name="attend",
    )(q, x)


def local(queries, keys, values):
    q = queries.reshape(ROWS, HEADS, GROUP, WIDTH)
    k = keys.reshape(ROWS * HEADS, WIDTH)
    v = values.reshape(ROWS * HEADS, WIDTH)
    q_all, x = gather(q, k, v)
    out, peak, norm = attend(q_all.reshape(-1, WIDTH), x.reshape(2, 2 * WIN, HALF, WIDTH))
    return out.reshape(1, 2 * HALF, GROUP, WIDTH), peak, norm


def solution(mesh):
    spec = P("ctx", "head", None, None)
    out_specs = (P("ctx", None, "head", None), P("head", "ctx", None), P("head", "ctx", None))
    return jax.shard_map(local, mesh=mesh, in_specs=(spec, spec, spec), out_specs=out_specs, check_vma=False)
```

```python
import functools
import math

import jax
import jax.numpy as jnp
from jax import lax
from jax.experimental import pallas as pl
from jax.experimental.pallas import tpu as pltpu
from jax.sharding import PartitionSpec as P

MESH = pl.DeviceIdType.MESH
HALF = 128
ROWS = 64
HEADS = 4
GROUP = 8
WIDTH = 128
BLOCK = 128
PAIRS = 256
WIN = 8


def gather_kernel(q_ref, k_ref, v_ref, q_out, x_out, wide, stage,
                  q_send, q_recv, q_own, s_send, s_recv, s_own, e_send, c_send, b_send, d_send, x_recv, w_send,
                  r_recv, r_send, relay, ready):
    c = lax.axis_index("ctx")
    h = lax.axis_index("head")
    core = lax.rem(c, 2)
    place = lax.rem(c, BLOCK)
    back = BLOCK - place
    crosser = back <= 7
    over = c >= BLOCK
    across = lax.select(over, c - BLOCK, c + BLOCK)
    base = lax.select(over, BLOCK, 0)
    x_core = lax.select(back == 7, 0, lax.rem(back, 2))
    x_j = lax.select(back == 7, 7, back + lax.rem(back, 2))
    near = place < 2
    last = place >= BLOCK - 2
    sibling = c + 1 - 2 * core

    def both(j):
        return (over & (c - j >= BLOCK - 3)) | (c < 4)

    def both_next(j):
        return (over & (c - j >= BLOCK - 3)) | (c < 2)

    def wrapped(pair):
        return lax.rem(pair + PAIRS, PAIRS)

    bar = pltpu.get_barrier_semaphore()

    def greet(pair, head):
        pl.semaphore_signal(bar, inc=1, device_id=(pair, head), device_id_type=MESH)

    for s in range(1, HEADS):
        greet(c, lax.rem(h + s, HEADS))
    greet(sibling, h)

    @pl.when(jnp.logical_not(near))
    def _():
        greet(c - 2, h)

        @pl.when(core == 0)
        def _():
            greet(c - 1, h)

    @pl.when(crosser)
    def _():
        for r in range(HEADS):
            greet(across, r)
        greet(base + x_core, h)

    for n, ref in enumerate((k_ref, v_ref)):
        wide[n] = ref[...].astype(jnp.float32)
    for n in range(2):
        for head in range(HEADS):
            stage[n, head] = wide[n, pl.ds(head, ROWS, stride=HEADS), :].astype(jnp.bfloat16)

    one, none = jnp.int32(1), jnp.int32(0)
    targets = (4 + lax.select(last, none, one) + lax.select(last | (core == 0), none, one)
               + lax.select(crosser, one, none) * 4 + lax.select(near, one, none) * (4 - core))
    pl.semaphore_wait(bar, targets)

    @pl.when(near)
    def _():
        for j in (2, 4, 6, 7):
            @pl.when((j != 7) | (core == 0))
            def _():
                pl.semaphore_signal(ready, inc=1, device_id=(wrapped(c - j + BLOCK), h), device_id_type=MESH)

    def remote(src, dst, send, recv, pair, head):
        return pltpu.make_async_remote_copy(src_ref=src, dst_ref=dst, send_sem=send, recv_sem=recv,
                                            device_id=(pair, head), device_id_type=MESH)

    def own_rows(head):
        return x_out.at[:, head // 2, 0, pl.ds(lax.rem(head, 2) * ROWS, ROWS), :]

    kv_copies = []
    for s in (3, 2, 1):
        to = lax.rem(h + s, HEADS)
        copy = remote(stage.at[:, to], own_rows(h), s_send.at[s], s_recv.at[h], c, to)
        copy.start()
        kv_copies.append(copy)
    kv_own = pltpu.make_async_copy(stage.at[:, h], own_rows(h), s_own)
    kv_own.start()

    half_to = lax.select(over, 1 - h // 2, h // 2)

    def cross_copy(to):
        return remote(stage.at[:, to], relay.at[:, half_to, pl.ds(lax.rem(h, 2) * ROWS, ROWS), :],
                      w_send.at[to], r_recv.at[half_to], across, to)

    def relay_copy(half):
        return remote(relay.at[:, half], x_out.at[:, half, x_j], r_send.at[half], x_recv.at[x_j, half],
                      base + x_core, h)

    crosses = crosser & (over | (back <= 3) | (h < 2))

    @pl.when(crosses)
    def _():
        for to in range(HEADS):
            cross_copy(to).start()

    q_copies = []
    for s in (3, 2, 1):
        to = lax.rem(h + s, HEADS)
        copy = remote(q_ref.at[:, to], q_out.at[h], q_send.at[s], q_recv.at[h], c, to)
        copy.start()
        q_copies.append(copy)
    q_mine = pltpu.make_async_copy(q_ref.at[:, h], q_out.at[h], q_own)
    q_mine.start()

    kv_own.wait()

    def arrive(head):
        @pl.when(h != head)
        def _():
            remote(stage.at[:, head], own_rows(head), e_send, s_recv.at[head], c, h).wait_recv()

    def block(half, j):
        return x_out.at[:, half, j]

    def along(j, half):
        return remote(block(half, j), block(half, j + 2), c_send.at[j // 2, half], x_recv.at[j + 2, half],
                      wrapped(c + 2), h)

    def beside(j, half):
        j_to = j + 1 - 2 * core
        return remote(block(half, j), block(half, j_to), b_send.at[j // 2, half], x_recv.at[j_to, half], sibling, h)

    def ahead(half):
        return remote(block(half, 6), block(half, 7), d_send.at[half], x_recv.at[7, half], wrapped(c + 1), h)

    def landed(j, half):
        remote(block(half, j), block(half, j), e_send, x_recv.at[j, half], c, h).wait_recv()

    def seen(half, where):
        return where if half else True

    def relays(half):
        return crosser & seen(half, jnp.logical_not(over) | (back <= 3))

    def chain(j, half, act):
        if j < 6:
            @pl.when(jnp.logical_not(last) & seen(half, both_next(j)))
            def _():
                act(along(j, half))
        else:
            @pl.when(jnp.logical_not(last) & (core == 1) & seen(half, both_next(j)))
            def _():
                act(ahead(half))

        @pl.when(seen(half, both(j)) & ((core == 0) | (j > 0)))
        def _():
            act(beside(j, half))

    for j in (0, 2, 4, 6):
        for half in range(2):
            if j:
                @pl.when(seen(half, both(j)))
                def _():
                    landed(j, half)
            else:
                arrive(2 * half)
                arrive(2 * half + 1)
            chain(j, half, lambda copy: copy.start())
        if j == 0:
            @pl.when(crosser)
            def _():
                pl.semaphore_wait(ready, 1)

            for half in range(2):
                @pl.when(relays(half))
                def _():
                    remote(relay.at[:, half], relay.at[:, half], e_send, r_recv.at[half], c, h).wait_recv()
                    relay_copy(half).start()
    for j in (1, 3, 5, 7):
        for half in range(2):
            @pl.when(seen(half, both(j)))
            def _():
                landed(j, half)
    for s in (1, 2, 3):
        head = lax.rem(h + s, HEADS)
        remote(q_ref.at[:, head], q_out.at[head], e_send, q_recv.at[head], c, h).wait_recv()
    q_mine.wait()
    for copy in kv_copies + q_copies:
        copy.wait_send()

    @pl.when(crosses)
    def _():
        for to in range(HEADS):
            cross_copy(to).wait_send()

    for half in range(2):
        @pl.when(relays(half))
        def _():
            relay_copy(half).wait_send()

    for half in range(2):
        for j in (0, 2, 4, 6):
            chain(j, half, lambda copy: copy.wait_send())


def gather(q, k, v):
    dma = pltpu.SemaphoreType.DMA
    any_space = pl.BlockSpec(memory_space=pl.ANY)
    vmem = pl.BlockSpec(memory_space=pltpu.VMEM)
    return pl.pallas_call(
        gather_kernel,
        out_shape=(
            jax.ShapeDtypeStruct((HEADS, ROWS, GROUP, WIDTH), jnp.bfloat16),
            jax.ShapeDtypeStruct((2, 2, WIN, HALF, WIDTH), jnp.bfloat16),
        ),
        in_specs=[any_space, vmem, vmem],
        out_specs=(any_space, any_space),
        scratch_shapes=[
            pltpu.VMEM((2, ROWS * HEADS, WIDTH), jnp.float32),
            pltpu.VMEM((2, HEADS, ROWS, WIDTH), jnp.bfloat16),
            dma((4,)), dma((4,)), dma(()), dma((4,)), dma((4,)), dma(()), dma(()), dma((3, 2)), dma((4, 2)), dma((2,)),
            dma((8, 2)), dma((4,)), dma((2,)), dma((2,)),
            pltpu.VMEM((2, 2, HALF, WIDTH), jnp.bfloat16),
            pltpu.SemaphoreType.REGULAR,
        ],
        compiler_params=pltpu.CompilerParams(collective_id=0, has_side_effects=True),
        name="gather",
    )(q, k, v)


CHUNK = 256
TOKENS = CHUNK // GROUP
SCALE = 1.0 / math.sqrt(WIDTH)
LOG2E = math.log2(math.e)
LOW = -1e30


def nt_dot(a, b):
    return lax.dot_general(a, b, (((1,), (1,)), ((), ())), preferred_element_type=jnp.float32)


def attend_kernel(q_ref, x_ref, o_ref, m_ref, l_ref, stats):
    step = pl.program_id(0)
    half_steps = HALF // TOKENS
    c = lax.axis_index("ctx")
    token0 = lax.rem(step, half_steps) * TOKENS
    half = step // half_steps
    upper = c >= BLOCK
    place = lax.rem(c, BLOCK)
    special = place < 4
    q = q_ref[...]

    @pl.when(step == 0)
    def _():
        stats[...] = jnp.zeros_like(stats)

    def causal():
        row = token0 + lax.broadcasted_iota(jnp.int32, (CHUNK, HALF), 0) // GROUP
        return lax.broadcasted_iota(jnp.int32, (CHUNK, HALF), 1) <= row

    def put_stats(peak, norm):
        lane = lax.broadcasted_iota(jnp.int32, (TOKENS, GROUP, HALF), 2)
        want = token0 + lax.broadcasted_iota(jnp.int32, (TOKENS, GROUP, HALF), 0)
        hit = lane == want
        for n, value in enumerate((peak, norm)):
            wide = jnp.broadcast_to(value, (CHUNK, HALF)).reshape(TOKENS, GROUP, HALF)
            stats[n, half] += jnp.sum(jnp.where(hit, wide, 0.0), axis=0)

    def whole(diagonal, *ranges):
        pieces = [(diagonal, diagonal + 1), *(r for r in ranges if r[1] > r[0])]
        s = []
        for n, (a, b) in enumerate(pieces):
            one = nt_dot(q, x_ref[0, a:b].reshape(-1, WIDTH))
            s.append(one if n else jnp.where(causal(), one, LOW))
        peak = functools.reduce(jnp.maximum, [jnp.max(one, axis=1, keepdims=True) for one in s])
        norm, out = 0.0, 0.0
        for one, (a, b) in zip(s, pieces):
            p = jnp.exp2((one - peak) * (SCALE * LOG2E))
            norm += jnp.sum(p, axis=1, keepdims=True)
            out += jnp.dot(p.astype(jnp.bfloat16), x_ref[1, a:b].reshape(-1, WIDTH),
                           preferred_element_type=jnp.float32)
        o_ref[...] = out
        put_stats(peak * SCALE, norm)

    cases = {(0, None): ([(1, WIN)], [(0, WIN)]), (1, None): ([(1, 2 * WIN)], [])}
    for two in range(0, WIN, 2):
        cases[0, two // 2] = ([(1, two + 1)], [(0, WIN), (WIN + two + 1, 2 * WIN)])
        cases[1, two // 2] = ([(1, WIN + two + 1)], [(two + 1, WIN)])
    for (side, at), by_half in cases.items():
        here = (upper == (side == 1)) & (jnp.logical_not(special) if at is None else place == at)
        for which, ranges in enumerate(by_half):
            @pl.when(here & (half == which))
            def _():
                whole(which * WIN, *ranges)

    @pl.when(step == 2 * half_steps - 1)
    def _():
        for n, ref in enumerate((m_ref, l_ref)):
            for side in range(2):
                for g in range(GROUP):
                    ref[g, :, pl.ds(side * HALF, HALF)] = stats[n, side, pl.ds(g, 1), :]


def attend(q, x):
    rows = q.shape[0]
    return pl.pallas_call(
        attend_kernel,
        grid=(rows // CHUNK,),
        out_shape=(
            jax.ShapeDtypeStruct((rows, WIDTH), jnp.float32),
            jax.ShapeDtypeStruct((GROUP, 1, 2 * HALF), jnp.float32),
            jax.ShapeDtypeStruct((GROUP, 1, 2 * HALF), jnp.float32),
        ),
        in_specs=[
            pl.BlockSpec((CHUNK, WIDTH), lambda i: (i, 0)),
            pl.BlockSpec((2, 2 * WIN, HALF, WIDTH), lambda i: (0, 0, 0, 0)),
        ],
        out_specs=(
            pl.BlockSpec((CHUNK, WIDTH), lambda i: (i, 0)),
            pl.BlockSpec((GROUP, 1, 2 * HALF), lambda i: (0, 0, 0)),
            pl.BlockSpec((GROUP, 1, 2 * HALF), lambda i: (0, 0, 0)),
        ),
        scratch_shapes=[
            pltpu.VMEM((2, 2, GROUP, HALF), jnp.float32),
        ],
        name="attend",
    )(q, x)


def local(queries, keys, values):
    q = queries.reshape(ROWS, HEADS, GROUP, WIDTH)
    k = keys.reshape(ROWS * HEADS, WIDTH)
    v = values.reshape(ROWS * HEADS, WIDTH)
    q_all, x = gather(q, k, v)
    out, peak, norm = attend(q_all.reshape(-1, WIDTH), x.reshape(2, 2 * WIN, HALF, WIDTH))
    return out.reshape(1, 2 * HALF, GROUP, WIDTH), peak, norm


def solution(mesh):
    spec = P("ctx", "head", None, None)
    out_specs = (P("ctx", None, "head", None), P("head", "ctx", None), P("head", "ctx", None))
    return jax.shard_map(local, mesh=mesh, in_specs=(spec, spec, spec), out_specs=out_specs, check_vma=False)
```

```python
import functools
import math

import jax
import jax.numpy as jnp
from jax import lax
from jax.experimental import pallas as pl
from jax.experimental.pallas import tpu as pltpu
from jax.sharding import PartitionSpec as P

MESH = pl.DeviceIdType.MESH
HALF = 128
ROWS = 64
HEADS = 4
GROUP = 8
WIDTH = 128
BLOCK = 128
PAIRS = 256
WIN = 8


def gather_kernel(q_ref, k_ref, v_ref, q_out, x_out, wide, stage,
                  q_send, q_recv, q_own, s_send, s_recv, s_own, e_send, c_send, b_send, d_send, x_recv, w_send,
                  r_recv, r_send, relay, ready, go):
    c = lax.axis_index("ctx")
    h = lax.axis_index("head")
    core = lax.rem(c, 2)
    place = lax.rem(c, BLOCK)
    back = BLOCK - place
    crosser = back <= 7
    over = c >= BLOCK
    across = lax.select(over, c - BLOCK, c + BLOCK)
    base = lax.select(over, BLOCK, 0)
    x_core = lax.select(back == 7, 0, lax.rem(back, 2))
    x_j = lax.select(back == 7, 7, back + lax.rem(back, 2))
    near = place < 2
    last = place >= BLOCK - 2
    sibling = c + 1 - 2 * core

    def both(j):
        return (over & (c - j >= BLOCK - 3)) | ((c < 2) & (j > c)) | ((c < 4) & (j >= c + 3))

    def both_next(j):
        return (over & (c - j >= BLOCK - 3)) | ((c < 2) & (j >= c + 3))

    def wrapped(pair):
        return lax.rem(pair + PAIRS, PAIRS)

    bar = pltpu.get_barrier_semaphore()

    def greet(pair, head):
        pl.semaphore_signal(bar, inc=1, device_id=(pair, head), device_id_type=MESH)

    for s in range(1, HEADS):
        greet(c, lax.rem(h + s, HEADS))
    greet(sibling, h)

    @pl.when(jnp.logical_not(near))
    def _():
        greet(c - 2, h)

        @pl.when(core == 0)
        def _():
            greet(c - 1, h)

    @pl.when(crosser)
    def _():
        greet(base + x_core, h)

        @pl.when(jnp.logical_not(over))
        def _():
            for r in range(HEADS):
                greet(across, r)

    for n, ref in enumerate((k_ref, v_ref)):
        wide[n] = ref[...].astype(jnp.float32)
    for n in range(2):
        for head in range(HEADS):
            stage[n, head] = wide[n, pl.ds(head, ROWS, stride=HEADS), :].astype(jnp.bfloat16)

    one, none = jnp.int32(1), jnp.int32(0)
    targets = (4 + lax.select(last, none, one) + lax.select(last | (core == 0), none, one)
               + lax.select(crosser & over, one, none) * 4 + lax.select(near, one, none) * (4 - core))
    pl.semaphore_wait(bar, targets)

    @pl.when(crosser & over)
    def _():
        for r in range(HEADS):
            pl.semaphore_signal(go.at[h], inc=1, device_id=(across, r), device_id_type=MESH)

    @pl.when(near)
    def _():
        for j in (2, 4, 6, 7):
            @pl.when((j != 7) | (core == 0))
            def _():
                pl.semaphore_signal(ready, inc=1, device_id=(wrapped(c - j + BLOCK), h), device_id_type=MESH)

    def remote(src, dst, send, recv, pair, head):
        return pltpu.make_async_remote_copy(src_ref=src, dst_ref=dst, send_sem=send, recv_sem=recv,
                                            device_id=(pair, head), device_id_type=MESH)

    def own_rows(head):
        return x_out.at[:, head // 2, 0, pl.ds(lax.rem(head, 2) * ROWS, ROWS), :]

    kv_copies = []
    for s in (3, 2, 1):
        to = lax.rem(h + s, HEADS)
        copy = remote(stage.at[:, to], own_rows(h), s_send.at[s], s_recv.at[h], c, to)
        copy.start()
        kv_copies.append(copy)
    kv_own = pltpu.make_async_copy(stage.at[:, h], own_rows(h), s_own)
    kv_own.start()

    half_to = lax.select(over, 1 - h // 2, h // 2)

    def cross_copy(to):
        return remote(stage.at[:, to], relay.at[:, half_to, pl.ds(lax.rem(h, 2) * ROWS, ROWS), :],
                      w_send.at[to], r_recv.at[half_to], across, to)

    def relay_copy(half):
        return remote(relay.at[:, half], x_out.at[:, half, x_j], r_send.at[half], x_recv.at[x_j, half],
                      base + x_core, h)

    crosses = crosser & (over | (back <= 3) | (h < 2))

    @pl.when(crosses & over)
    def _():
        for to in range(HEADS):
            cross_copy(to).start()

    q_copies = []
    for s in (3, 2, 1):
        to = lax.rem(h + s, HEADS)
        copy = remote(q_ref.at[:, to], q_out.at[h], q_send.at[s], q_recv.at[h], c, to)
        copy.start()
        q_copies.append(copy)
    q_mine = pltpu.make_async_copy(q_ref.at[:, h], q_out.at[h], q_own)
    q_mine.start()

    kv_own.wait()

    def arrive(head):
        @pl.when(h != head)
        def _():
            remote(stage.at[:, head], own_rows(head), e_send, s_recv.at[head], c, h).wait_recv()

    def block(half, j):
        return x_out.at[:, half, j]

    def along(j, half):
        return remote(block(half, j), block(half, j + 2), c_send.at[j // 2, half], x_recv.at[j + 2, half],
                      wrapped(c + 2), h)

    def beside(j, half):
        j_to = j + 1 - 2 * core
        return remote(block(half, j), block(half, j_to), b_send.at[j // 2, half], x_recv.at[j_to, half], sibling, h)

    def ahead(half):
        return remote(block(half, 6), block(half, 7), d_send.at[half], x_recv.at[7, half], wrapped(c + 1), h)

    def landed(j, half):
        remote(block(half, j), block(half, j), e_send, x_recv.at[j, half], c, h).wait_recv()

    def seen(half, where):
        return where if half else True

    def relays(half):
        return crosser & seen(half, jnp.logical_not(over) | (back <= 3))

    def chain(j, half, act):
        if j < 6:
            @pl.when(jnp.logical_not(last) & seen(half, both_next(j)))
            def _():
                act(along(j, half))
        else:
            @pl.when(jnp.logical_not(last) & (core == 1) & seen(half, both_next(j)))
            def _():
                act(ahead(half))

        @pl.when(seen(half, both(j)) & ((core == 0) | (j > 0)))
        def _():
            act(beside(j, half))

    for j in (0, 2, 4, 6):
        for half in range(2):
            if j:
                @pl.when(seen(half, both(j)))
                def _():
                    landed(j, half)
            else:
                arrive(2 * half)
                arrive(2 * half + 1)
            chain(j, half, lambda copy: copy.start())
        if j == 0:
            @pl.when(crosser & jnp.logical_not(over))
            def _():
                for to in range(HEADS):
                    pl.semaphore_wait(go.at[to], 1)

                    @pl.when(crosses)
                    def _():
                        cross_copy(to).start()

            @pl.when(crosser)
            def _():
                pl.semaphore_wait(ready, 1)

            for half in (1, 0):
                @pl.when(relays(half))
                def _():
                    remote(relay.at[:, half], relay.at[:, half], e_send, r_recv.at[half], c, h).wait_recv()
                    relay_copy(half).start()
    for j in (1, 3, 5, 7):
        for half in range(2):
            @pl.when(seen(half, both(j)))
            def _():
                landed(j, half)
    for s in (1, 2, 3):
        head = lax.rem(h + s, HEADS)
        remote(q_ref.at[:, head], q_out.at[head], e_send, q_recv.at[head], c, h).wait_recv()
    q_mine.wait()
    for copy in kv_copies + q_copies:
        copy.wait_send()

    @pl.when(crosses)
    def _():
        for to in range(HEADS):
            cross_copy(to).wait_send()

    for half in range(2):
        @pl.when(relays(half))
        def _():
            relay_copy(half).wait_send()

    for half in range(2):
        for j in (0, 2, 4, 6):
            chain(j, half, lambda copy: copy.wait_send())


def gather(q, k, v):
    dma = pltpu.SemaphoreType.DMA
    any_space = pl.BlockSpec(memory_space=pl.ANY)
    vmem = pl.BlockSpec(memory_space=pltpu.VMEM)
    return pl.pallas_call(
        gather_kernel,
        out_shape=(
            jax.ShapeDtypeStruct((HEADS, ROWS, GROUP, WIDTH), jnp.bfloat16),
            jax.ShapeDtypeStruct((2, 2, WIN, HALF, WIDTH), jnp.bfloat16),
        ),
        in_specs=[any_space, vmem, vmem],
        out_specs=(any_space, any_space),
        scratch_shapes=[
            pltpu.VMEM((2, ROWS * HEADS, WIDTH), jnp.float32),
            pltpu.VMEM((2, HEADS, ROWS, WIDTH), jnp.bfloat16),
            dma((4,)), dma((4,)), dma(()), dma((4,)), dma((4,)), dma(()), dma(()), dma((3, 2)), dma((4, 2)), dma((2,)),
            dma((8, 2)), dma((4,)), dma((2,)), dma((2,)),
            pltpu.VMEM((2, 2, HALF, WIDTH), jnp.bfloat16),
            pltpu.SemaphoreType.REGULAR,
            pltpu.SemaphoreType.REGULAR((HEADS,)),
        ],
        compiler_params=pltpu.CompilerParams(collective_id=0, has_side_effects=True),
        name="gather",
    )(q, k, v)


CHUNK = 512
TOKENS = CHUNK // GROUP
PIECE = 4
SCALE = 1.0 / math.sqrt(WIDTH)
LOG2E = math.log2(math.e)
LOW = -1e30


def nt_dot(a, b):
    return lax.dot_general(a, b, (((1,), (1,)), ((), ())), preferred_element_type=jnp.float32)


def attend_kernel(q_ref, x_ref, o_ref, m_ref, l_ref, stats):
    step = pl.program_id(0)
    half_steps = HALF // TOKENS
    c = lax.axis_index("ctx")
    token0 = lax.rem(step, half_steps) * TOKENS
    half = step // half_steps
    upper = c >= BLOCK
    place = lax.rem(c, BLOCK)
    special = place < 4
    q = q_ref[...]

    @pl.when(step == 0)
    def _():
        stats[...] = jnp.zeros_like(stats)

    def causal():
        row = token0 + lax.broadcasted_iota(jnp.int32, (CHUNK, HALF), 0) // GROUP
        return lax.broadcasted_iota(jnp.int32, (CHUNK, HALF), 1) <= row

    def put_stats(peak, norm):
        lane = lax.broadcasted_iota(jnp.int32, (TOKENS, GROUP, HALF), 2)
        want = token0 + lax.broadcasted_iota(jnp.int32, (TOKENS, GROUP, HALF), 0)
        hit = lane == want
        for n, value in enumerate((peak, norm)):
            wide = jnp.broadcast_to(value, (CHUNK, HALF)).reshape(TOKENS, GROUP, HALF)
            stats[n, half] += jnp.sum(jnp.where(hit, wide, 0.0), axis=0)

    def whole(diagonal, *ranges):
        cut = [(x, min(x + PIECE, b)) for a, b in ranges for x in range(a, b, PIECE)]
        pieces = [(diagonal, diagonal + 1), *cut]
        s = []
        for n, (a, b) in enumerate(pieces):
            one = nt_dot(q, x_ref[0, a:b].reshape(-1, WIDTH))
            s.append(one if n else jnp.where(causal(), one, LOW))
        peak = functools.reduce(jnp.maximum, [jnp.max(one, axis=1, keepdims=True) for one in s])
        norm, out = 0.0, 0.0
        for one, (a, b) in zip(s, pieces):
            p = jnp.exp2((one - peak) * (SCALE * LOG2E))
            norm += jnp.sum(p, axis=1, keepdims=True)
            out += jnp.dot(p.astype(jnp.bfloat16), x_ref[1, a:b].reshape(-1, WIDTH),
                           preferred_element_type=jnp.float32)
        o_ref[...] = out
        put_stats(peak * SCALE, norm)

    cases = {(0, None): ([(1, WIN)], [(0, WIN)]), (1, None): ([(1, 2 * WIN)], [])}
    for two in range(0, WIN, 2):
        cases[0, two // 2] = ([(1, two + 1)], [(0, WIN), (WIN + two + 1, 2 * WIN)])
        cases[1, two // 2] = ([(1, WIN + two + 1)], [(two + 1, WIN)])
    for (side, at), by_half in cases.items():
        here = (upper == (side == 1)) & (jnp.logical_not(special) if at is None else place == at)
        for which, ranges in enumerate(by_half):
            @pl.when(here & (half == which))
            def _():
                whole(which * WIN, *ranges)

    @pl.when(step == 2 * half_steps - 1)
    def _():
        for n, ref in enumerate((m_ref, l_ref)):
            for side in range(2):
                for g in range(GROUP):
                    ref[g, :, pl.ds(side * HALF, HALF)] = stats[n, side, pl.ds(g, 1), :]


def attend(q, x):
    rows = q.shape[0]
    return pl.pallas_call(
        attend_kernel,
        grid=(rows // CHUNK,),
        out_shape=(
            jax.ShapeDtypeStruct((rows, WIDTH), jnp.float32),
            jax.ShapeDtypeStruct((GROUP, 1, 2 * HALF), jnp.float32),
            jax.ShapeDtypeStruct((GROUP, 1, 2 * HALF), jnp.float32),
        ),
        in_specs=[
            pl.BlockSpec((CHUNK, WIDTH), lambda i: (i, 0)),
            pl.BlockSpec((2, 2 * WIN, HALF, WIDTH), lambda i: (0, 0, 0, 0)),
        ],
        out_specs=(
            pl.BlockSpec((CHUNK, WIDTH), lambda i: (i, 0)),
            pl.BlockSpec((GROUP, 1, 2 * HALF), lambda i: (0, 0, 0)),
            pl.BlockSpec((GROUP, 1, 2 * HALF), lambda i: (0, 0, 0)),
        ),
        scratch_shapes=[
            pltpu.VMEM((2, 2, GROUP, HALF), jnp.float32),
        ],
        name="attend",
    )(q, x)


def local(queries, keys, values):
    q = queries.reshape(ROWS, HEADS, GROUP, WIDTH)
    k = keys.reshape(ROWS * HEADS, WIDTH)
    v = values.reshape(ROWS * HEADS, WIDTH)
    q_all, x = gather(q, k, v)
    out, peak, norm = attend(q_all.reshape(-1, WIDTH), x.reshape(2, 2 * WIN, HALF, WIDTH))
    return out.reshape(1, 2 * HALF, GROUP, WIDTH), peak, norm


def solution(mesh):
    spec = P("ctx", "head", None, None)
    out_specs = (P("ctx", None, "head", None), P("head", "ctx", None), P("head", "ctx", None))
    return jax.shard_map(local, mesh=mesh, in_specs=(spec, spec, spec), out_specs=out_specs, check_vma=False)
```

```python
import functools
import math

import jax
import jax.numpy as jnp
from jax import lax
from jax.experimental import pallas as pl
from jax.experimental.pallas import tpu as pltpu
from jax.sharding import PartitionSpec as P

MESH = pl.DeviceIdType.MESH
HALF = 128
ROWS = 64
HEADS = 4
GROUP = 8
WIDTH = 128
BLOCK = 128
PAIRS = 256
WIN = 8


def gather_kernel(q_ref, k_ref, v_ref, q_out, x_out, wide, stage,
                  q_send, q_recv, q_own, s_send, s_recv, s_own, e_send, c_send, b_send, d_send, x_recv, w_send,
                  r_recv, r_send, relay, ready, go):
    c = lax.axis_index("ctx")
    h = lax.axis_index("head")
    core = lax.rem(c, 2)
    place = lax.rem(c, BLOCK)
    back = BLOCK - place
    crosser = back <= 7
    over = c >= BLOCK
    across = lax.select(over, c - BLOCK, c + BLOCK)
    base = lax.select(over, BLOCK, 0)
    x_core = lax.select(back == 7, 0, lax.rem(back, 2))
    x_j = lax.select(back == 7, 7, back + lax.rem(back, 2))
    near = place < 2
    last = place >= BLOCK - 2
    sibling = c + 1 - 2 * core

    def both(j):
        return (over & (c - j >= BLOCK - 3)) | ((c < 2) & (j > c)) | ((c < 4) & (j >= c + 3))

    def both_next(j):
        return (over & (c - j >= BLOCK - 3)) | ((c < 2) & (j >= c + 3))

    def wrapped(pair):
        return lax.rem(pair + PAIRS, PAIRS)

    bar = pltpu.get_barrier_semaphore()

    def greet(pair, head):
        pl.semaphore_signal(bar, inc=1, device_id=(pair, head), device_id_type=MESH)

    for s in range(1, HEADS):
        greet(c, lax.rem(h + s, HEADS))
    greet(sibling, h)

    @pl.when(jnp.logical_not(near))
    def _():
        greet(c - 2, h)

        @pl.when(core == 0)
        def _():
            greet(c - 1, h)

    @pl.when(crosser)
    def _():
        greet(base + x_core, h)

        @pl.when(jnp.logical_not(over))
        def _():
            for r in range(HEADS):
                greet(across, r)

    for n, ref in enumerate((k_ref, v_ref)):
        wide[n] = ref[...].astype(jnp.float32)
    for n in range(2):
        for head in range(HEADS):
            stage[n, head] = wide[n, pl.ds(head, ROWS, stride=HEADS), :].astype(jnp.bfloat16)

    one, none = jnp.int32(1), jnp.int32(0)
    targets = (4 + lax.select(last, none, one) + lax.select(last | (core == 0), none, one)
               + lax.select(crosser & over, one, none) * 4 + lax.select(near, one, none) * (4 - core))
    pl.semaphore_wait(bar, targets)

    @pl.when(crosser & over)
    def _():
        for r in range(HEADS):
            pl.semaphore_signal(go.at[h], inc=1, device_id=(across, r), device_id_type=MESH)

    @pl.when(near)
    def _():
        for j in (2, 4, 6, 7):
            @pl.when((j != 7) | (core == 0))
            def _():
                pl.semaphore_signal(ready, inc=1, device_id=(wrapped(c - j + BLOCK), h), device_id_type=MESH)

    def remote(src, dst, send, recv, pair, head):
        return pltpu.make_async_remote_copy(src_ref=src, dst_ref=dst, send_sem=send, recv_sem=recv,
                                            device_id=(pair, head), device_id_type=MESH)

    def own_rows(head):
        return x_out.at[:, head // 2, 0, pl.ds(lax.rem(head, 2) * ROWS, ROWS), :]

    kv_copies = []
    for s in (3, 2, 1):
        to = lax.rem(h + s, HEADS)
        copy = remote(stage.at[:, to], own_rows(h), s_send.at[s], s_recv.at[h], c, to)
        copy.start()
        kv_copies.append(copy)
    kv_own = pltpu.make_async_copy(stage.at[:, h], own_rows(h), s_own)
    kv_own.start()

    half_to = lax.select(over, 1 - h // 2, h // 2)

    def cross_copy(to):
        return remote(stage.at[:, to], relay.at[:, half_to, pl.ds(lax.rem(h, 2) * ROWS, ROWS), :],
                      w_send.at[to], r_recv.at[half_to], across, to)

    def relay_copy(half):
        return remote(relay.at[:, half], x_out.at[:, half, x_j], r_send.at[half], x_recv.at[x_j, half],
                      base + x_core, h)

    crosses = crosser & (over | (back <= 3) | (h < 2))

    @pl.when(crosses & over)
    def _():
        for to in range(HEADS):
            cross_copy(to).start()

    q_copies = []
    for s in (3, 2, 1):
        to = lax.rem(h + s, HEADS)
        copy = remote(q_ref.at[:, to], q_out.at[h], q_send.at[s], q_recv.at[h], c, to)
        copy.start()
        q_copies.append(copy)
    q_mine = pltpu.make_async_copy(q_ref.at[:, h], q_out.at[h], q_own)
    q_mine.start()

    kv_own.wait()

    def arrive(head):
        @pl.when(h != head)
        def _():
            remote(stage.at[:, head], own_rows(head), e_send, s_recv.at[head], c, h).wait_recv()

    def block(half, j):
        return x_out.at[:, half, j]

    def along(j, half):
        return remote(block(half, j), block(half, j + 2), c_send.at[j // 2, half], x_recv.at[j + 2, half],
                      wrapped(c + 2), h)

    def beside(j, half):
        j_to = j + 1 - 2 * core
        return remote(block(half, j), block(half, j_to), b_send.at[j // 2, half], x_recv.at[j_to, half], sibling, h)

    def ahead(half):
        return remote(block(half, 6), block(half, 7), d_send.at[half], x_recv.at[7, half], wrapped(c + 1), h)

    def landed(j, half):
        remote(block(half, j), block(half, j), e_send, x_recv.at[j, half], c, h).wait_recv()

    def seen(half, where):
        return where if half else True

    def relays(half):
        return crosser & seen(half, jnp.logical_not(over) | (back <= 3))

    def chain(j, half, act):
        if j < 6:
            @pl.when(jnp.logical_not(last) & seen(half, both_next(j)))
            def _():
                act(along(j, half))
        else:
            @pl.when(jnp.logical_not(last) & (core == 1) & seen(half, both_next(j)))
            def _():
                act(ahead(half))

        @pl.when(seen(half, both(j)) & ((core == 0) | (j > 0)))
        def _():
            act(beside(j, half))

    for j in (0, 2, 4, 6):
        for half in range(2):
            if j:
                @pl.when(seen(half, both(j)))
                def _():
                    landed(j, half)
            else:
                arrive(2 * half)
                arrive(2 * half + 1)
            chain(j, half, lambda copy: copy.start())
        if j == 0:
            @pl.when(crosser & jnp.logical_not(over))
            def _():
                for to in range(HEADS):
                    pl.semaphore_wait(go.at[to], 1)

                    @pl.when(crosses)
                    def _():
                        cross_copy(to).start()

            @pl.when(crosser)
            def _():
                pl.semaphore_wait(ready, 1)

            for half in (1, 0):
                @pl.when(relays(half))
                def _():
                    remote(relay.at[:, half], relay.at[:, half], e_send, r_recv.at[half], c, h).wait_recv()
                    relay_copy(half).start()
    for j in (1, 3, 5, 7):
        for half in range(2):
            @pl.when(seen(half, both(j)))
            def _():
                landed(j, half)
    for s in (1, 2, 3):
        head = lax.rem(h + s, HEADS)
        remote(q_ref.at[:, head], q_out.at[head], e_send, q_recv.at[head], c, h).wait_recv()
    q_mine.wait()
    for copy in kv_copies + q_copies:
        copy.wait_send()

    @pl.when(crosses)
    def _():
        for to in range(HEADS):
            cross_copy(to).wait_send()

    for half in range(2):
        @pl.when(relays(half))
        def _():
            relay_copy(half).wait_send()

    for half in range(2):
        for j in (0, 2, 4, 6):
            chain(j, half, lambda copy: copy.wait_send())


def gather(q, k, v):
    dma = pltpu.SemaphoreType.DMA
    any_space = pl.BlockSpec(memory_space=pl.ANY)
    vmem = pl.BlockSpec(memory_space=pltpu.VMEM)
    return pl.pallas_call(
        gather_kernel,
        out_shape=(
            jax.ShapeDtypeStruct((HEADS, ROWS, GROUP, WIDTH), jnp.bfloat16),
            jax.ShapeDtypeStruct((2, 2, WIN, HALF, WIDTH), jnp.bfloat16),
        ),
        in_specs=[pl.BlockSpec(memory_space=pltpu.HBM), vmem, vmem],
        out_specs=(any_space, any_space),
        scratch_shapes=[
            pltpu.VMEM((2, ROWS * HEADS, WIDTH), jnp.float32),
            pltpu.VMEM((2, HEADS, ROWS, WIDTH), jnp.bfloat16),
            dma((4,)), dma((4,)), dma(()), dma((4,)), dma((4,)), dma(()), dma(()), dma((3, 2)), dma((4, 2)), dma((2,)),
            dma((8, 2)), dma((4,)), dma((2,)), dma((2,)),
            pltpu.VMEM((2, 2, HALF, WIDTH), jnp.bfloat16),
            pltpu.SemaphoreType.REGULAR,
            pltpu.SemaphoreType.REGULAR((HEADS,)),
        ],
        compiler_params=pltpu.CompilerParams(collective_id=0, has_side_effects=True, vmem_limit_bytes=8 << 20),
        name="gather",
    )(q, k, v)


CHUNK = 512
TOKENS = CHUNK // GROUP
PIECE = 4
SCALE = 1.0 / math.sqrt(WIDTH)
LOG2E = math.log2(math.e)
LOW = -1e30


def nt_dot(a, b):
    return lax.dot_general(a, b, (((1,), (1,)), ((), ())), preferred_element_type=jnp.float32)


def attend_kernel(q_ref, x_ref, o_ref, m_ref, l_ref, stats):
    step = pl.program_id(0)
    half_steps = HALF // TOKENS
    c = lax.axis_index("ctx")
    token0 = lax.rem(step, half_steps) * TOKENS
    half = step // half_steps
    upper = c >= BLOCK
    place = lax.rem(c, BLOCK)
    special = place < 4
    q = q_ref[...]

    @pl.when(step == 0)
    def _():
        stats[...] = jnp.zeros_like(stats)

    def causal():
        row = token0 + lax.broadcasted_iota(jnp.int32, (CHUNK, HALF), 0) // GROUP
        return lax.broadcasted_iota(jnp.int32, (CHUNK, HALF), 1) <= row

    def put_stats(peak, norm):
        lane = lax.broadcasted_iota(jnp.int32, (TOKENS, GROUP, HALF), 2)
        want = token0 + lax.broadcasted_iota(jnp.int32, (TOKENS, GROUP, HALF), 0)
        hit = lane == want
        for n, value in enumerate((peak, norm)):
            wide = jnp.broadcast_to(value, (CHUNK, HALF)).reshape(TOKENS, GROUP, HALF)
            stats[n, half] += jnp.sum(jnp.where(hit, wide, 0.0), axis=0)

    def whole(diagonal, *ranges):
        cut = [(x, min(x + PIECE, b)) for a, b in ranges for x in range(a, b, PIECE)]
        pieces = [(diagonal, diagonal + 1), *cut]
        s = []
        for n, (a, b) in enumerate(pieces):
            one = nt_dot(q, x_ref[0, a:b].reshape(-1, WIDTH))
            s.append(one if n else jnp.where(causal(), one, LOW))
        peak = functools.reduce(jnp.maximum, [jnp.max(one, axis=1, keepdims=True) for one in s])
        norm, out = 0.0, 0.0
        for one, (a, b) in zip(s, pieces):
            p = jnp.exp2((one - peak) * (SCALE * LOG2E))
            norm += jnp.sum(p, axis=1, keepdims=True)
            out += jnp.dot(p.astype(jnp.bfloat16), x_ref[1, a:b].reshape(-1, WIDTH),
                           preferred_element_type=jnp.float32)
        o_ref[...] = out
        put_stats(peak * SCALE, norm)

    cases = {(0, None): ([(1, WIN)], [(0, WIN)]), (1, None): ([(1, 2 * WIN)], [])}
    for two in range(0, WIN, 2):
        cases[0, two // 2] = ([(1, two + 1)], [(0, WIN), (WIN + two + 1, 2 * WIN)])
        cases[1, two // 2] = ([(1, WIN + two + 1)], [(two + 1, WIN)])
    for (side, at), by_half in cases.items():
        here = (upper == (side == 1)) & (jnp.logical_not(special) if at is None else place == at)
        for which, ranges in enumerate(by_half):
            @pl.when(here & (half == which))
            def _():
                whole(which * WIN, *ranges)

    @pl.when(step == 2 * half_steps - 1)
    def _():
        for n, ref in enumerate((m_ref, l_ref)):
            for side in range(2):
                for g in range(GROUP):
                    ref[g, :, pl.ds(side * HALF, HALF)] = stats[n, side, pl.ds(g, 1), :]


def attend(q, x):
    rows = q.shape[0]
    return pl.pallas_call(
        attend_kernel,
        grid=(rows // CHUNK,),
        out_shape=(
            jax.ShapeDtypeStruct((rows, WIDTH), jnp.float32),
            jax.ShapeDtypeStruct((GROUP, 1, 2 * HALF), jnp.float32),
            jax.ShapeDtypeStruct((GROUP, 1, 2 * HALF), jnp.float32),
        ),
        in_specs=[
            pl.BlockSpec((CHUNK, WIDTH), lambda i: (i, 0)),
            pl.BlockSpec((2, 2 * WIN, HALF, WIDTH), lambda i: (0, 0, 0, 0)),
        ],
        out_specs=(
            pl.BlockSpec((CHUNK, WIDTH), lambda i: (i, 0)),
            pl.BlockSpec((GROUP, 1, 2 * HALF), lambda i: (0, 0, 0)),
            pl.BlockSpec((GROUP, 1, 2 * HALF), lambda i: (0, 0, 0)),
        ),
        scratch_shapes=[
            pltpu.VMEM((2, 2, GROUP, HALF), jnp.float32),
        ],
        compiler_params=pltpu.CompilerParams(vmem_limit_bytes=48 << 20),
        name="attend",
    )(q, x)


def local(queries, keys, values):
    q = queries.reshape(ROWS, HEADS, GROUP, WIDTH)
    k = keys.reshape(ROWS * HEADS, WIDTH)
    v = values.reshape(ROWS * HEADS, WIDTH)
    q_all, x = gather(q, k, v)
    out, peak, norm = attend(q_all.reshape(-1, WIDTH), x.reshape(2, 2 * WIN, HALF, WIDTH))
    return out.reshape(1, 2 * HALF, GROUP, WIDTH), peak, norm


def solution(mesh):
    spec = P("ctx", "head", None, None)
    out_specs = (P("ctx", None, "head", None), P("head", "ctx", None), P("head", "ctx", None))
    return jax.shard_map(local, mesh=mesh, in_specs=(spec, spec, spec), out_specs=out_specs, check_vma=False)
```
